32 devices in a mesh: heads: 16 (over z, y, core), width: 2 (over x).
Axes of the slice: x: 2, y: 2, z: 4, core: 2. Of those that a mesh axis runs over, the one named last changes fastest.
Arguments:
- out_grad: bfloat16 [512, 7168], P('heads', 'width'), may hold values from -24 to 24
- w_out: float32 [4096, 7168], P('heads', 'width'), may hold values from -0.09375 to 0.09375
- row_moment: float32 [4096], P('heads'), may hold values from 4 to 400
- col_moment: float32 [7168], P('width'), may hold values from 4 to 400
- queries: bfloat16 [512, 6144], P('width', 'heads'), may hold values from -240 to 240
- latent: bfloat16 [512, 512], P('width'), may hold values from -6 to 6
- key_rope: bfloat16 [512, 64], P('width'), may hold values from -4 to 4
- w_kv_up: bfloat16 [512, 8192], P(None, 'heads'), may hold values from -0.25 to 0.25
- doc_lengths: int32 [2, 4], P('width'), may hold values from 1 to 160, 256 in all within a row
Outputs:
- weight_update: float32 [4096, 7168], P('heads', 'width')
- query_grad: bfloat16 [512, 6144], P('width', 'heads')
- latent_grad: float32 [512, 576], P('width', 'heads')
- kv_up_grad: float32 [512, 8192], P('width', 'heads')
The draws below stay inside these ranges and needn't reach their ends.
Inputs may be any that keep to these rules, and one draw needn't show every extreme that they name: `doc_lengths`: row p holds the lengths of the 4 documents packed in order into pack p; they sum to 256 and the longest in every row is exactly 160.
All inputs are finite; a program needn't handle non-finite values.
Results may differ from the reference program's by a relative error of at most 0.0088.
Values may be sent and summed in bfloat16 or wider, within the bound.
No kernel may reach another device: no remote copies, remote signals or barrier semaphores. Data moves between devices by JAX's collectives and lax.ppermute only.
A program may use at most 64 MiB of HBM per device.

```python
import math
import jax
import jax.numpy as jnp
import numpy as np
from jax import lax

D = 7168
HEADS = 32
VD = 128
NOPE = 128
ROPE = 64
KV = 512
PACK = 256
DOCS_PACK = 4
DOC_MOST = 160
TOKENS = 512
N_WIDTH = 2


def rope_keys(key):
    base_draw = jax.random.normal(jax.random.fold_in(key, 11), (TOKENS, ROPE), jnp.float32)
    return jnp.clip(base_draw, -4.0, 4.0)


def draw_key_rope(key, part):
    return rope_keys(key).astype(jnp.bfloat16)


def draw_queries(key, part):
    head_width = NOPE + ROPE
    base_draw = jax.random.normal(jax.random.fold_in(key, 23), (TOKENS, HEADS, head_width), jnp.float32)
    base_draw = jnp.clip(base_draw, -4.0, 4.0)
    return base_draw.reshape(TOKENS, HEADS * head_width).astype(jnp.bfloat16)


def steps_of(own_key, extent, shards, least, high):
    gain = 1.0
    for dim, parts in shards:
        heights = jax.random.uniform(jax.random.fold_in(jax.random.fold_in(own_key, 6), dim), (parts,), jnp.float32, least / len(shards), high / len(shards))
        gain = gain * jnp.repeat(jnp.exp(heights), extent[dim] // parts).reshape((-1,) + (1,) * (len(extent) - 1 - dim))
    return gain


def split_up(number_of, total, reach, skew):
    weights = [(1 << 20) // math.isqrt(grade ** skew) + 1 for grade in range(2, number_of + 1)]
    surplus, given = total - reach - (number_of - 1), [1] * (number_of - 1)
    while surplus > 0:
        movable = [i for i in range(number_of - 1) if given[i] < reach]
        pool, left = sum([weights[i] for i in movable]), surplus
        for i in movable:
            more = min(reach - given[i], max(1, left * weights[i] // pool), surplus)
            given[i] = given[i] + more
            surplus = surplus - more
    return np.array([reach] + given)


def uneven_parts(stream_key, number_of, total, bound, skew):
    if number_of == 2:
        one = jax.random.randint(stream_key, (), max(1, total - bound), min(bound, total - 1) + 1)
        return jnp.stack([one, total - one])
    sizes = jnp.asarray(split_up(number_of, total, bound, skew), jnp.int32)
    twos = (number_of - 1) // 2
    source_of, sink = sizes[1:1 + 2 * twos:2], sizes[2:2 + 2 * twos:2]
    room = jnp.minimum(source_of - 1, bound - sink)
    passed = jax.random.randint(jax.random.fold_in(stream_key, 1), (twos,), 0, 1 << 20) % (room + 1)
    sizes = sizes.at[1:1 + 2 * twos:2].set(source_of - passed).at[2:2 + 2 * twos:2].set(sink + passed)
    return sizes[jax.random.permutation(jax.random.fold_in(stream_key, 2), number_of)]


def centred(stream_key, dims, deviation, reach, shards=(), held_as=jnp.bfloat16):
    array = deviation * jax.random.normal(stream_key, dims, jnp.float32)
    if shards:
        array = array * steps_of(stream_key, dims, shards, -0.22, 0.18)
    return jnp.clip(array, -reach, reach).astype(held_as)


def setup_inputs(seed: int = 0) -> dict:
    seeds = jax.random.split(jax.random.key(seed), 10)
    return {
        "out_grad": centred(seeds[0], (TOKENS, D), 4.0, 24.0, ((0, 16), (1, 2))),
        "w_out": centred(seeds[1], (HEADS * VD, D), (HEADS * VD) ** -0.5, 0.09375, ((0, 16), (1, 2)), jnp.float32),
        "row_moment": jnp.clip(jnp.exp(math.log(400.0) - 4.6051702 * jax.random.uniform(seeds[2], (HEADS * VD,), jnp.float32) ** steps_of(seeds[2], (HEADS * VD,), ((0, 16),), -0.2, 0.2)), 4.0, 400.0),
        "col_moment": jnp.clip(jnp.exp(math.log(400.0) - 4.6051702 * jax.random.uniform(seeds[3], (D,), jnp.float32) ** steps_of(seeds[3], (D,), ((0, 2),), -0.2, 0.2)), 4.0, 400.0),
        "queries": draw_queries(jax.random.fold_in(seeds[9], 71), 0),
        "latent": centred(seeds[5], (TOKENS, KV), 1.0, 6.0, ((0, 2),)),
        "key_rope": draw_key_rope(jax.random.fold_in(seeds[9], 71), 0),
        "w_kv_up": centred(seeds[7], (KV, HEADS * (NOPE + VD)), KV ** -0.5, 0.25, ((1, 16),)),
        "doc_lengths": jax.vmap(lambda own: uneven_parts(own, DOCS_PACK, PACK, DOC_MOST, 2))(jax.random.split(seeds[8], N_WIDTH)).reshape((N_WIDTH, DOCS_PACK)).astype(jnp.int32),
    }


moment_decay = 0.9
update_eps = 1e-06

def doc_mask(lengths, length):
    doc_ends = jnp.cumsum(lengths).astype(jnp.int32)
    position = jnp.arange(length, dtype=jnp.int32)
    document = lax.optimization_barrier(jnp.sum((position[:, None] >= doc_ends[None, :]).astype(jnp.int32), axis=1))
    return (document[:, None] == document[None, :]) & (position[None, :] <= position[:, None])

def forward_pack(queries, latent, key_rope, w_kv_up, allowed):
    length = queries.shape[0]
    n_heads = w_kv_up.shape[1] // (NOPE + VD)
    scale_factor = (NOPE + ROPE) ** (-0.5)
    key_value = jnp.dot(latent, w_kv_up, preferred_element_type=jnp.float32).astype(jnp.bfloat16)
    key_value = key_value.reshape(length, n_heads, NOPE + VD)
    key_nope = key_value[:, :, :NOPE]
    values = key_value[:, :, NOPE:]
    query_heads = queries.reshape(length, n_heads, NOPE + ROPE)
    scores = jnp.einsum('ihd,jhd->hij', query_heads[:, :, :NOPE].astype(jnp.float32), key_nope.astype(jnp.float32))
    scores = scores + jnp.einsum('ihd,jd->hij', query_heads[:, :, NOPE:].astype(jnp.float32), key_rope.astype(jnp.float32))
    scores = scores * scale_factor
    masked = jnp.where(allowed[None], scores, -jnp.inf)
    highest = lax.optimization_barrier(jnp.max(masked, axis=2, keepdims=True))
    weights = jnp.exp(masked - highest)
    prob_full = weights / lax.optimization_barrier(jnp.sum(weights, axis=2, keepdims=True))
    probs_half = prob_full.astype(jnp.bfloat16)
    attended = jnp.einsum('hij,jhd->ihd', probs_half.astype(jnp.float32), values.astype(jnp.float32))
    attended = attended.astype(jnp.bfloat16).reshape(length, n_heads * VD)
    return (query_heads, key_nope, values, prob_full, probs_half, attended)

def backward_pack(states, attn_half, latent, key_rope, w_kv_up):
    query_heads, key_nope, values, prob_full, probs_half, attended = states
    length = query_heads.shape[0]
    n_heads = query_heads.shape[1]
    scale_factor = (NOPE + ROPE) ** (-0.5)
    grad_heads = attn_half.reshape(length, n_heads, VD).astype(jnp.float32)
    row_delta = lax.optimization_barrier(jnp.sum(grad_heads * attended.reshape(length, n_heads, VD).astype(jnp.float32), axis=2)).T
    prob_grad = jnp.einsum('ihd,jhd->hij', grad_heads, values.astype(jnp.float32))
    score_grad = (prob_full * (prob_grad - row_delta[:, :, None]) * scale_factor).astype(jnp.bfloat16)
    score_wide = score_grad.astype(jnp.float32)
    nope_grad = jnp.einsum('hij,jhd->ihd', score_wide, key_nope.astype(jnp.float32))
    rotary_grad = jnp.einsum('hij,jd->ihd', score_wide, key_rope.astype(jnp.float32))
    query_grad = jnp.concatenate([nope_grad, rotary_grad], axis=2).astype(jnp.bfloat16)
    query_grad = query_grad.reshape(length, n_heads * (NOPE + ROPE))
    key_nope_grad = jnp.einsum('hij,ihd->jhd', score_wide, query_heads[:, :, :NOPE].astype(jnp.float32))
    rope_grad = jnp.einsum('hij,ihd->jd', score_wide, query_heads[:, :, NOPE:].astype(jnp.float32))
    value_grad = jnp.einsum('hij,ihd->jhd', probs_half.astype(jnp.float32), grad_heads)
    kv_grad = jnp.concatenate([key_nope_grad, value_grad], axis=2).astype(jnp.bfloat16)
    kv_grad = kv_grad.reshape(length, n_heads * (NOPE + VD))
    latent_part = jnp.dot(kv_grad, w_kv_up.T, preferred_element_type=jnp.float32)
    latent_term = jnp.concatenate([latent_part, rope_grad], axis=1)
    kv_term = jnp.dot(latent.T, kv_grad, preferred_element_type=jnp.float32)
    return (query_grad, latent_term, kv_term)

def reference(out_grad, w_out, row_moment, col_moment, queries, latent, key_rope, w_kv_up, doc_lengths):
    length = PACK
    saved_states = []
    attended_list = []
    for pack_index in range(N_WIDTH):
        first = pack_index * length
        allowed = doc_mask(doc_lengths[pack_index], length)
        states = forward_pack(queries[first:first + length], latent[first:first + length], key_rope[first:first + length], w_kv_up, allowed)
        saved_states.append(states)
        attended_list.append(states[5])
    attended_whole = jnp.concatenate(attended_list, axis=0)
    w_half = w_out.astype(jnp.bfloat16)
    attn_half = jnp.dot(out_grad, w_half.T, preferred_element_type=jnp.float32).astype(jnp.bfloat16)
    gradient = jnp.dot(attended_whole.T, out_grad, preferred_element_type=jnp.float32)
    query_list = []
    latent_list = []
    kv_up_grad = jnp.zeros((KV, w_kv_up.shape[1]), jnp.float32)
    for pack_index in range(N_WIDTH):
        first = pack_index * length
        query_grad, latent_term, kv_term = backward_pack(saved_states[pack_index], attn_half[first:first + length], latent[first:first + length], key_rope[first:first + length], w_kv_up)
        query_list.append(query_grad)
        latent_list.append(latent_term)
        kv_up_grad = kv_up_grad + kv_term
    squares = gradient * gradient
    row_new = moment_decay * row_moment + (1.0 - moment_decay) * lax.optimization_barrier(jnp.mean(squares, axis=1))
    col_new = moment_decay * col_moment + (1.0 - moment_decay) * lax.optimization_barrier(jnp.mean(squares, axis=0))
    scaled = gradient / jnp.sqrt(row_new[:, None] * col_new[None, :])
    weight_update = scaled / jnp.sqrt(jnp.mean(scaled * scaled) + update_eps)
    return (weight_update, jnp.concatenate(query_list, axis=0), jnp.concatenate(latent_list, axis=0), kv_up_grad)
```

```python
import jax
import jax.numpy as jnp
from jax import lax
from jax.sharding import PartitionSpec as P

D = 7168
VD = 128
NOPE = 128
ROPE = 64


moment_decay = 0.9
update_eps = 1e-06


def xor_swap(x, axis, bit):
    size = lax.axis_size(axis)
    return lax.ppermute(x, axis, [(i, i ^ bit) for i in range(size)])


def bits_down(size):
    bits = []
    bit = size // 2
    while bit:
        bits.append(bit)
        bit //= 2
    return bits


def gather_xor(x, axis):
    size = lax.axis_size(axis)
    parts = {0: x}
    for bit in bits_down(size):
        for mask in list(parts):
            parts[mask | bit] = xor_swap(parts[mask], axis, bit)
    return [parts[mask] for mask in range(size)]


def reduce_scatter_xor(x, axis):
    size = lax.axis_size(axis)
    index = lax.axis_index(axis)
    bit = 1
    while bit < size:
        pairs = x.reshape((x.shape[0] // 2, 2) + x.shape[1:])
        own = (index // bit) % 2
        keep = lax.dynamic_index_in_dim(pairs, own, 1, keepdims=False)
        give = lax.dynamic_index_in_dim(pairs, 1 - own, 1, keepdims=False)
        x = keep + xor_swap(give.astype(jnp.bfloat16), axis, bit).astype(jnp.float32)
        bit *= 2
    return x[0]


def all_sum_xor(x, axis):
    bit = 1
    while bit < lax.axis_size(axis):
        x = x + xor_swap(x, axis, bit)
        bit *= 2
    return x


def scatter_sum_xor(x, axis):
    size = lax.axis_size(axis)
    return reduce_scatter_xor(x.reshape((size, x.shape[0] // size) + x.shape[1:]), axis)


def doc_mask(lengths, length):
    doc_ends = jnp.cumsum(lengths)
    position = jnp.arange(length, dtype=jnp.int32)
    document = jnp.sum((position[:, None] >= doc_ends[None, :]).astype(jnp.int32), axis=1)
    return (document[:, None] == document[None, :]) & (position[None, :] <= position[:, None])


def forward_pack(queries, latent, key_rope, w_kv_up, allowed):
    length = queries.shape[0]
    n_heads = w_kv_up.shape[1] // (NOPE + VD)
    scale_factor = (NOPE + ROPE) ** (-0.5)
    key_value = jnp.dot(latent, w_kv_up, preferred_element_type=jnp.float32).astype(jnp.bfloat16)
    key_value = key_value.reshape(length, n_heads, NOPE + VD)
    key_nope = key_value[:, :, :NOPE]
    values = key_value[:, :, NOPE:]
    query_heads = queries.reshape(length, n_heads, NOPE + ROPE)
    scores = jnp.einsum(
        "ihd,jhd->hij", query_heads[:, :, :NOPE], key_nope, preferred_element_type=jnp.float32
    )
    scores = scores + jnp.einsum(
        "ihd,jd->hij", query_heads[:, :, NOPE:], key_rope, preferred_element_type=jnp.float32
    )
    scores = scores * scale_factor
    masked = jnp.where(allowed[None], scores, -jnp.inf)
    highest = jnp.max(masked, axis=2, keepdims=True)
    weights = jnp.exp(masked - highest)
    prob_full = weights / jnp.sum(weights, axis=2, keepdims=True)
    probs_half = prob_full.astype(jnp.bfloat16)
    attended = jnp.einsum("hij,jhd->ihd", probs_half, values, preferred_element_type=jnp.float32)
    attended = attended.astype(jnp.bfloat16).reshape(length, n_heads * VD)
    return (query_heads, key_nope, values, prob_full, probs_half, attended)


def backward_pack(states, attn_half, key_rope, w_kv_up):
    query_heads, key_nope, values, prob_full, probs_half, attended = states
    length = query_heads.shape[0]
    n_heads = query_heads.shape[1]
    scale_factor = (NOPE + ROPE) ** (-0.5)
    grad_heads = attn_half.reshape(length, n_heads, VD)
    row_delta = jnp.sum(
        grad_heads.astype(jnp.float32) * attended.reshape(length, n_heads, VD).astype(jnp.float32),
        axis=2,
    ).T
    prob_grad = jnp.einsum("ihd,jhd->hij", grad_heads, values, preferred_element_type=jnp.float32)
    score_grad = (prob_full * (prob_grad - row_delta[:, :, None]) * scale_factor).astype(
        jnp.bfloat16
    )
    nope_grad = jnp.einsum("hij,jhd->ihd", score_grad, key_nope, preferred_element_type=jnp.float32)
    rotary_grad = jnp.einsum(
        "hij,jd->ihd", score_grad, key_rope, preferred_element_type=jnp.float32
    )
    query_grad = jnp.concatenate([nope_grad, rotary_grad], axis=2).astype(jnp.bfloat16)
    query_grad = query_grad.reshape(length, n_heads * (NOPE + ROPE))
    key_nope_grad = jnp.einsum(
        "hij,ihd->jhd", score_grad, query_heads[:, :, :NOPE], preferred_element_type=jnp.float32
    )
    rope_grad = jnp.einsum(
        "hij,ihd->dj", score_grad, query_heads[:, :, NOPE:], preferred_element_type=jnp.float32
    )
    value_grad = jnp.einsum(
        "hij,ihd->jhd", probs_half, grad_heads, preferred_element_type=jnp.float32
    )
    kv_grad = jnp.concatenate([key_nope_grad, value_grad], axis=2).astype(jnp.bfloat16)
    kv_grad = kv_grad.reshape(length, n_heads * (NOPE + VD))
    latent_part = lax.dot_general(
        w_kv_up, kv_grad, (((1,), (1,)), ((), ())), preferred_element_type=jnp.float32
    )
    latent_term = jnp.concatenate([latent_part, rope_grad], axis=0)
    return (query_grad, latent_term, kv_grad)


def on_device(
    out_grad, w_out, row_moment, col_moment, queries, latent, key_rope, w_kv_up, doc_lengths
):
    length = queries.shape[0]
    head_count = lax.axis_size("heads")
    head_index = lax.axis_index("heads")
    width_count = lax.axis_size("width")
    width_index = lax.axis_index("width")
    tokens = length * width_count
    parts = gather_xor(out_grad, "heads")
    grad_rows = jnp.concatenate(parts, axis=0)
    order = head_index ^ jnp.arange(head_count, dtype=jnp.int32)

    allowed = doc_mask(doc_lengths[0], length)
    states = forward_pack(queries, latent, key_rope, w_kv_up, allowed)
    attended = states[5]
    attended_parts = gather_xor(attended, "width")
    order_width = width_index ^ jnp.arange(width_count, dtype=jnp.int32)
    attended_all = jnp.stack(attended_parts)[order_width].reshape(
        head_count, tokens // head_count, attended.shape[1]
    )
    w_half = w_out.astype(jnp.bfloat16)
    attn_part = lax.dot_general(
        grad_rows, w_half, (((1,), (1,)), ((), ())), preferred_element_type=jnp.float32
    )
    attn_part = attn_part.reshape(head_count, tokens // head_count, -1)[order]
    attn_grad = scatter_sum_xor(attn_part.reshape(tokens, -1), "width")
    attn_half = attn_grad.astype(jnp.bfloat16)
    gradient = lax.dot_general(
        attended_all[order].reshape(tokens, -1),
        grad_rows,
        (((0,), (0,)), ((), ())),
        preferred_element_type=jnp.float32,
    )
    query_grad, latent_term, kv_grad = backward_pack(states, attn_half, key_rope, w_kv_up)
    latent_grad = scatter_sum_xor(latent_term, "heads").T
    kv_up_grad = scatter_sum_xor(
        lax.dot_general(
            latent, kv_grad, (((0,), (0,)), ((), ())), preferred_element_type=jnp.float32
        ),
        "width",
    )
    squares = gradient * gradient
    rows_total = gradient.shape[0] * head_count
    row_sum = all_sum_xor(jnp.sum(squares, axis=1), "width")
    row_new = moment_decay * row_moment + (1.0 - moment_decay) * row_sum / D
    col_pair = jnp.stack(
        [jnp.sum(squares, axis=0), jnp.sum(squares * (1.0 / row_new)[:, None], axis=0)]
    )
    col_pair = all_sum_xor(col_pair, "heads")
    col_new = moment_decay * col_moment + (1.0 - moment_decay) * col_pair[0] / rows_total
    mean_square = all_sum_xor(jnp.sum(col_pair[1] / col_new), "width") / (rows_total * D)
    row_factor = lax.rsqrt(row_new)
    col_factor = lax.rsqrt(col_new) * lax.rsqrt(mean_square + update_eps)
    weight_update = gradient * row_factor[:, None] * col_factor[None, :]
    return (weight_update, query_grad, latent_grad, kv_up_grad)


def solution(mesh):
    in_specs = (
        P("heads", "width"),
        P("heads", "width"),
        P("heads"),
        P("width"),
        P("width", "heads"),
        P("width", None),
        P("width", None),
        P(None, "heads"),
        P("width", None),
    )
    out_specs = (P("heads", "width"), P("width", "heads"), P("width", "heads"), P("width", "heads"))
    return jax.shard_map(
        on_device, mesh=mesh, in_specs=in_specs, out_specs=out_specs, check_vma=False
    )
```
